32 devices in a mesh: tm: 8 (over z, x), video: 4 (over y, core).
Axes of the slice: x: 2, y: 2, z: 4, core: 2. Of those that a mesh axis runs over, the one named last changes fastest.
Arguments:
- frames: bfloat16 [4, 2048, 512], P('video', 'tm'), may hold values from -6 to 6
- dilated_weight: bfloat16 [3, 512, 512], replicated, may hold values from -0.15625 to 0.15625
- dilated_bias: float32 [512], replicated, may hold values from -3 to 3
- head_matrix: bfloat16 [512, 256], replicated, may hold values from -0.25 to 0.25
- narrations: bfloat16 [1024, 256], P('video'), may hold values from -256 to 256
- narration_counts: int32 [4], replicated, may hold values from 128 to 256, as said below
- narration_spans: int32 [4, 256, 2], P('video'), may hold values from 0 to 2048, as said below
Outputs:
- loss: float32 [], replicated
- dil_grad: float32 [3, 512, 512], P(None, 'tm')
- head_grad: float32 [512, 256], P('tm')
- bias_grad: float32 [512], replicated
- input_gradient: bfloat16 [4, 2048, 512], P('video', 'tm')
The draws below stay inside these ranges and needn't reach their ends.
Inputs may be any that keep to these rules, and one draw needn't show every extreme that they name: `narration_counts`: the number of live narration slots of each video; some video has all 256. Narration j of a video covers frames narration_spans[v, j, 0] up to but excluding narration_spans[v, j, 1], one frame or more, inside the j-th of the 256 equal runs of 8 frames; spans of slots at or above the count are not live.
All inputs are finite; a program needn't handle non-finite values.
Results may differ from the reference program's by a relative error of at most 0.025.
Values may be sent and summed in bfloat16 or wider, within the bound.
A program may use at most 64 MiB of HBM per device.

```python
import math
import jax
import jax.numpy as jnp
from jax import lax

CONV_CHANNELS = 512
E = 256
T_DEV = 256
NARR = 256
SHIFT_N = 2
VIDEOS = 4
FRAMES = 2048


def draw_narrations(key, part):
    keys = jax.random.split(key, 1)
    base = jax.random.normal(keys[0], (VIDEOS, NARR, E), jnp.float32)
    return jnp.clip(base, -256.0, 256.0).reshape(VIDEOS * NARR, E).astype(jnp.bfloat16)


def draw_narration_counts(key, part):
    keys = jax.random.split(key, 2)
    counts = NARR - jax.random.randint(keys[0], (VIDEOS,), 0, NARR // 2 + 1)
    full = jax.random.randint(keys[1], (), 0, VIDEOS)
    return jnp.where(jnp.arange(VIDEOS) == full, NARR, counts).astype(jnp.int32)


def draw_narration_spans(key, part):
    keys = jax.random.split(key, 2)
    slot = FRAMES // NARR
    index = jnp.arange(NARR, dtype=jnp.int32)
    longest = jnp.maximum(1, slot * (NARR + 2 * index) // (3 * NARR))
    span_len = jax.random.randint(keys[0], (VIDEOS, NARR), 1, longest[None, :] + 1)
    offset = jax.random.randint(keys[1], (VIDEOS, NARR), 0, slot - span_len + 1)
    start = index[None, :] * slot + offset
    return jnp.stack([start, start + span_len], axis=2).astype(jnp.int32)


def spiked(array, stream_key, source, target, shards_of, factor):
    owner, partner = [(jnp.arange(array.shape[dim]) // (array.shape[dim] // shards_of)).reshape([-1 if axis == dim else 1 for axis in range(array.ndim)]) for dim in (source, target)]
    chosen = jax.random.permutation(stream_key, shards_of)[partner]
    strong = (owner == chosen) | (owner == (partner + shards_of // 2) % shards_of)
    return jnp.where(strong, factor * array, array)


def shard_levels(key, dims, pieces, smallest, largest):
    level = 1.0
    for position, shards_of in pieces:
        draws = jax.random.uniform(jax.random.fold_in(jax.random.fold_in(key, 6), position), (shards_of,), jnp.float32, smallest / len(pieces), largest / len(pieces))
        level = level * jnp.repeat(jnp.exp(draws), dims[position] // shards_of).reshape((-1,) + (1,) * (len(dims) - 1 - position))
    return level


def centred(rng, shape, scale, most, cuts=(), kind=jnp.bfloat16):
    gain = shard_levels(rng, shape, cuts, -0.22, 0.18) if cuts else 1.0
    array = jax.random.normal(rng, shape, jnp.float32) * scale * gain
    return jnp.minimum(jnp.maximum(array, -most), most).astype(kind)


def gaussian_with(key, shape, width, most, cuts, heavy, kind=jnp.bfloat16):
    result = width * jax.random.normal(key, shape, jnp.float32)
    if cuts:
        result = result * shard_levels(key, shape, cuts, -0.22, 0.18)
    return jnp.clip(spiked(result, jax.random.fold_in(key, 3), *heavy), -most, most).astype(kind)


def setup_inputs(seed: int = 0) -> dict:
    key_of = jax.random.split(jax.random.key(seed), 8)
    frames = gaussian_with(key_of[0], (VIDEOS, FRAMES, CONV_CHANNELS), 1.0, 6.0, ((0, 4), (1, 8)), (1, 2, 8, 2.0))
    dilated_weight = centred(key_of[1], (3, CONV_CHANNELS, CONV_CHANNELS), (3 * CONV_CHANNELS) ** -0.5, 0.15625)
    dilated_bias = centred(key_of[2], (CONV_CHANNELS,), 0.5, 3.0, (), jnp.float32)
    head_matrix = centred(key_of[3], (CONV_CHANNELS, E), CONV_CHANNELS ** -0.5, 0.25)
    narrations = draw_narrations(jax.random.fold_in(key_of[7], 71), 0)
    narration_counts = draw_narration_counts(jax.random.fold_in(key_of[7], 71), 0)
    narration_spans = draw_narration_spans(jax.random.fold_in(key_of[7], 71), 0)
    return {"frames": frames, "dilated_weight": dilated_weight, "dilated_bias": dilated_bias, "head_matrix": head_matrix, "narrations": narrations, "narration_counts": narration_counts, "narration_spans": narration_spans}


logit_scale = 0.0625


def contracted_rows(left, right):
    return lax.dot_general(left, right, (((0,), (0,)), ((), ())), preferred_element_type=jnp.float32)


def contracted_columns(left, right):
    return lax.dot_general(left, right, (((1,), (1,)), ((), ())), preferred_element_type=jnp.float32)


def reference(frames, dilated_weight, dilated_bias, head_matrix, narrations, narration_counts, narration_spans):
    reach = SHIFT_N * T_DEV
    slots = jnp.arange(NARR, dtype=jnp.int32)
    live = slots[None, :] < narration_counts[:, None]
    valid = live.reshape(-1)
    span_lengths = jnp.where(live, narration_spans[:, :, 1] - narration_spans[:, :, 0], 0).astype(jnp.float32)
    label_total = jnp.sum(span_lengths)
    factor = (VIDEOS * FRAMES) / label_total
    block = math.gcd(FRAMES, 4096)

    def one_video(video_number):
        present_tap = lax.dynamic_index_in_dim(frames, video_number, 0, keepdims=False)
        padded = jnp.pad(present_tap, ((reach, reach), (0, 0)))
        preceding_tap = padded[:FRAMES]
        following_tap = padded[2 * reach:]
        hidden_state = (jnp.dot(preceding_tap, dilated_weight[0], preferred_element_type=jnp.float32)
                  + jnp.dot(present_tap, dilated_weight[1], preferred_element_type=jnp.float32)
                  + jnp.dot(following_tap, dilated_weight[2], preferred_element_type=jnp.float32) + dilated_bias)
        layer_out = (present_tap.astype(jnp.float32) + jnp.maximum(hidden_state, 0.0)).astype(jnp.bfloat16)
        embedded = jnp.dot(layer_out, head_matrix, preferred_element_type=jnp.float32).astype(jnp.bfloat16)
        spans = lax.dynamic_index_in_dim(narration_spans, video_number, 0, keepdims=False)
        own_count = lax.dynamic_index_in_dim(narration_counts, video_number, 0, keepdims=False)
        own_start = (video_number * NARR).astype(jnp.int32)

        def loss_block(index):
            first = (index * block).astype(jnp.int32)
            rows = lax.dynamic_slice_in_dim(embedded, first, block, 0)
            scores = logit_scale * contracted_columns(rows, narrations)
            masked = jnp.where(valid[None, :], scores, -jnp.inf)
            highest = jnp.max(masked, axis=1, keepdims=True)
            log_total = highest + jnp.log(jnp.sum(jnp.exp(masked - highest), axis=1, keepdims=True))
            positions = first + jnp.arange(block, dtype=jnp.int32)
            member = ((positions[:, None] >= spans[None, :, 0]) & (positions[:, None] < spans[None, :, 1])
                      & (slots[None, :] < own_count)).astype(jnp.float32)
            labeled = jnp.sum(member, axis=1)
            own_scores = lax.dynamic_slice_in_dim(scores, own_start, NARR, 1)
            part_loss = jnp.sum(labeled * log_total[:, 0]) - jnp.sum(member * own_scores)
            probs = jnp.exp(masked - log_total) * labeled[:, None]
            own_grad = lax.dynamic_slice_in_dim(probs, own_start, NARR, 1) - member
            score_grad = lax.dynamic_update_slice_in_dim(probs, own_grad, own_start, 1)
            score_grad = (score_grad * factor).astype(jnp.bfloat16)
            embed_rows = (logit_scale * jnp.dot(score_grad, narrations, preferred_element_type=jnp.float32)).astype(jnp.bfloat16)
            return part_loss, embed_rows

        loss_values, embed_parts = lax.map(loss_block, jnp.arange(FRAMES // block, dtype=jnp.int32))
        embed_grad = embed_parts.reshape(FRAMES, E)
        head_portion = contracted_rows(layer_out, embed_grad)
        output_gradient = contracted_columns(embed_grad, head_matrix).astype(jnp.bfloat16)
        preactivation_gradient = jnp.where(hidden_state > 0.0, output_gradient.astype(jnp.float32), 0.0).astype(jnp.bfloat16)
        bias_portion = jnp.sum(preactivation_gradient.astype(jnp.float32), axis=0)
        dilated_portion = jnp.stack([contracted_rows(preceding_tap, preactivation_gradient), contracted_rows(present_tap, preactivation_gradient),
                              contracted_rows(following_tap, preactivation_gradient)])
        padded_grad = jnp.pad(preactivation_gradient, ((reach, reach), (0, 0)))
        preceding_gradient = padded_grad[:FRAMES]
        following_gradient = padded_grad[2 * reach:]
        input_portion = (output_gradient.astype(jnp.float32) + contracted_columns(preactivation_gradient, dilated_weight[1])
                      + contracted_columns(following_gradient, dilated_weight[0]) + contracted_columns(preceding_gradient, dilated_weight[2]))
        return jnp.sum(loss_values), dilated_portion, head_portion, bias_portion, input_portion.astype(jnp.bfloat16)

    loss_portions, dilated_portions, head_portions, bias_portions, input_gradient = lax.map(
        one_video, jnp.arange(VIDEOS, dtype=jnp.int32))
    loss = jnp.sum(loss_portions) / label_total
    return loss, jnp.sum(dilated_portions, axis=0), jnp.sum(head_portions, axis=0), jnp.sum(bias_portions, axis=0), input_gradient
```

```python
import functools

import jax
import jax.numpy as jnp
from jax import lax
from jax.experimental import pallas as pl
from jax.experimental.pallas import tpu as pltpu
from jax.sharding import PartitionSpec as P

SHIFT_N = 2


logit_scale = 0.0625


def passed_along(value, axis, steps):
    count = lax.axis_size(axis)
    first, last = (max(0, -steps), min(count, count - steps))
    return lax.ppermute(value, axis, [(source, source + steps) for source in range(first, last)])


def moved(values, offset):
    return passed_along(values, "tm", offset)


def moved_back(values, offset):
    return passed_along(values, "tm", offset)


def contracted_rows(left, right):
    return lax.dot_general(
        left, right, (((0,), (0,)), ((), ())), preferred_element_type=jnp.float32
    )


def contracted_columns(left, right):
    return lax.dot_general(
        left, right, (((1,), (1,)), ((), ())), preferred_element_type=jnp.float32
    )


def per_device(
    frames, dilated_weight, dilated_bias, head_matrix, narrations, narration_counts, narration_spans
):
    present_tap = frames[0]
    length = present_tap.shape[0]
    narr_local = narrations.shape[0]
    preceding_tap = moved(present_tap, SHIFT_N)
    following_tap = moved(present_tap, -SHIFT_N)
    middle_frames = jnp.dot(present_tap, dilated_weight[1], preferred_element_type=jnp.float32)
    hidden_state = (
        middle_frames
        + jnp.dot(preceding_tap, dilated_weight[0], preferred_element_type=jnp.float32)
        + jnp.dot(following_tap, dilated_weight[2], preferred_element_type=jnp.float32)
        + dilated_bias
    )
    layer_out = (present_tap.astype(jnp.float32) + jnp.maximum(hidden_state, 0.0)).astype(
        jnp.bfloat16
    )
    embedded = jnp.dot(layer_out, head_matrix, preferred_element_type=jnp.float32).astype(
        jnp.bfloat16
    )
    every_narr = lax.all_gather(narrations, "video", axis=0, tiled=True)
    scores = logit_scale * contracted_columns(embedded, every_narr)
    slots = jnp.arange(narr_local, dtype=jnp.int32)
    valid = (slots[None, :] < narration_counts[:, None]).reshape(-1)
    masked = jnp.where(valid[None, :], scores, -jnp.inf)
    highest = jnp.max(masked, axis=1, keepdims=True)
    log_total = highest + jnp.log(jnp.sum(jnp.exp(masked - highest), axis=1, keepdims=True))
    video_index = lax.axis_index("video")
    own_count = lax.dynamic_index_in_dim(narration_counts, video_index, 0, keepdims=False)
    spans = narration_spans[0]
    positions = lax.axis_index("tm") * length + jnp.arange(length, dtype=jnp.int32)
    member = (
        (positions[:, None] >= spans[None, :, 0])
        & (positions[:, None] < spans[None, :, 1])
        & (slots[None, :] < own_count)
    ).astype(jnp.float32)
    labeled = jnp.sum(member, axis=1)
    own_start = video_index * narr_local
    own_scores = lax.dynamic_slice_in_dim(scores, own_start, narr_local, 1)
    local_loss = jnp.sum(labeled * log_total[:, 0]) - jnp.sum(member * own_scores)
    span_lengths = jnp.where(slots < own_count, spans[:, 1] - spans[:, 0], 0).astype(jnp.float32)
    label_total = lax.psum(jnp.sum(span_lengths), "video")
    factor = length * lax.axis_size("tm") * lax.axis_size("video") / label_total
    probs = jnp.exp(masked - log_total) * labeled[:, None]
    own_grad = lax.dynamic_slice_in_dim(probs, own_start, narr_local, 1) - member
    score_grad = lax.dynamic_update_slice_in_dim(probs, own_grad, own_start, 1)
    score_grad = (score_grad * factor).astype(jnp.bfloat16)
    embed_grad = (
        logit_scale * jnp.dot(score_grad, every_narr, preferred_element_type=jnp.float32)
    ).astype(jnp.bfloat16)
    head_resident = contracted_rows(layer_out, embed_grad)
    output_gradient = contracted_columns(embed_grad, head_matrix).astype(jnp.bfloat16)
    preactivation_gradient = jnp.where(
        hidden_state > 0.0, output_gradient.astype(jnp.float32), 0.0
    ).astype(jnp.bfloat16)
    received_following = moved_back(preactivation_gradient, -SHIFT_N)
    received_preceding = moved_back(preactivation_gradient, SHIFT_N)
    bias_local = jnp.sum(preactivation_gradient.astype(jnp.float32), axis=0)
    dilated_resident = jnp.stack(
        [
            contracted_rows(preceding_tap, preactivation_gradient),
            contracted_rows(present_tap, preactivation_gradient),
            contracted_rows(following_tap, preactivation_gradient),
        ]
    )
    input_gradient = (
        output_gradient.astype(jnp.float32)
        + contracted_columns(preactivation_gradient, dilated_weight[1])
        + contracted_columns(received_following, dilated_weight[0])
        + contracted_columns(received_preceding, dilated_weight[2])
    )
    loss_total, bias_overall = lax.psum((local_loss, bias_local), ("tm", "video"))
    dilated_complete, head_complete = lax.psum((dilated_resident, head_resident), "video")
    dilated_fraction, head_fraction = (
        lax.psum_scatter(dilated_complete, "tm", scatter_dimension=1, tiled=True),
        lax.psum_scatter(head_complete[None], "tm", scatter_dimension=1, tiled=True),
    )
    loss = loss_total / label_total
    return (
        loss,
        dilated_fraction,
        head_fraction[0],
        bias_overall,
        input_gradient.astype(jnp.bfloat16)[None],
    )


MESH = pl.DeviceIdType.MESH
F32, BF16 = jnp.float32, jnp.bfloat16


def section_kernel(
    n, videos, parts,
    counts_ref, frames_ref, weight_ref, bias_ref, head_ref, narr_ref, spans_ref,
    dil_ref, head_out_ref, input_ref, small_ref,
    earlier, later, narr_all, spans_all, hidden, out_grad, pre, pre_next, pre_prev,
    small_send, small_recv, edge_send, edge_recv, gather_send, gather_recv,
    small_ssem, small_rsem, *buffers,
):
    tm, vid = lax.axis_index("tm"), lax.axis_index("video")
    runs = n // 2
    core, row = lax.rem(vid, 2), lax.div(vid, 2)
    side, deep = lax.rem(tm, 2), lax.div(tm, 2)
    across_core = {"tm": tm, "video": vid + 1 - 2 * core}
    across_row = {"tm": tm, "video": lax.rem(vid + 2, videos)}
    across_side = {"tm": tm + 1 - 2 * side, "video": vid}

    def at_run(step):
        return {"tm": lax.rem(tm + 2 * step, n), "video": vid}

    def at_video(step):
        return {"tm": tm, "video": lax.rem(vid + step, videos)}

    barrier = pltpu.get_barrier_semaphore()
    peers = [across_side] + [at_run(s) for s in range(1, runs)] + [at_video(s) for s in range(1, videos)]
    for peer in peers:
        pl.semaphore_signal(barrier, inc=1, device_id=peer, device_id_type=MESH)
    pl.semaphore_wait(barrier, len(peers))

    def remote(src, dst, ssem, rsem, peer):
        return pltpu.make_async_remote_copy(
            src_ref=src, dst_ref=dst, send_sem=ssem, recv_sem=rsem, device_id=peer, device_id_type=MESH
        )

    has_prev, has_next = tm >= SHIFT_N, tm < n - SHIFT_N
    up = {"tm": lax.rem(tm + SHIFT_N, n), "video": vid}
    down = {"tm": lax.rem(tm + n - SHIFT_N, n), "video": vid}
    frames_up = remote(frames_ref.at[0], earlier, edge_send.at[0], edge_recv.at[0], up)
    frames_down = remote(frames_ref.at[0], later, edge_send.at[1], edge_recv.at[1], down)
    pre_up = remote(pre, pre_prev, edge_send.at[2], edge_recv.at[2], up)
    pre_down = remote(pre, pre_next, edge_send.at[3], edge_recv.at[3], down)
    pl.when(has_next)(frames_up.start)
    pl.when(has_prev)(frames_down.start)
    gathers = []
    for step in range(1, videos):
        gathers.append(remote(spans_ref, spans_all.at[step - 1], gather_send.at[0, step - 1], gather_recv.at[0, step - 1], at_video(step)))
        gathers.append(remote(narr_ref, narr_all.at[step - 1], gather_send.at[1, step - 1], gather_recv.at[1, step - 1], at_video(step)))
    for copy in gathers:
        copy.start()

    def no_prev():
        earlier[...] = jnp.zeros_like(earlier)
        pre_prev[...] = jnp.zeros_like(pre_prev)

    def no_next():
        later[...] = jnp.zeros_like(later)
        pre_next[...] = jnp.zeros_like(pre_next)

    pl.when(jnp.logical_not(has_prev))(no_prev)
    pl.when(jnp.logical_not(has_next))(no_next)

    present = frames_ref[0]
    length = present.shape[0]
    slots_count = narr_ref.shape[0]
    hidden[...] = jnp.dot(present, weight_ref[1], preferred_element_type=F32) + bias_ref[...]
    slots = lax.broadcasted_iota(jnp.int32, (1, slots_count), 1)
    positions = tm * length + lax.broadcasted_iota(jnp.int32, (length, 1), 0)
    starts, ends = spans_ref[0:1, :], spans_ref[1:2, :]
    own_live = slots < counts_ref[vid]
    member = ((positions >= starts) & (positions < ends) & own_live).astype(F32)
    labeled = jnp.sum(member, axis=1, keepdims=True)

    def recv_up():
        frames_up.wait_recv()

    pl.when(has_prev)(recv_up)
    hidden[...] += jnp.dot(earlier[...], weight_ref[0], preferred_element_type=F32)
    pl.when(has_next)(frames_down.wait_recv)
    hidden[...] += jnp.dot(later[...], weight_ref[2], preferred_element_type=F32)
    layer_out = (present.astype(F32) + jnp.maximum(hidden[...], 0.0)).astype(BF16)
    embedded = jnp.dot(layer_out, head_ref[...], preferred_element_type=F32).astype(BF16)

    span_sum = jnp.where(own_live, (ends - starts).astype(F32), 0.0)
    narrs, masked = [], []
    for step in range(videos):
        if step:
            gathers[2 * (step - 1)].wait_recv()
            gathers[2 * (step - 1) + 1].wait_recv()
            live = slots < counts_ref[lax.rem(vid + videos - step, videos)]
            lengths = (spans_all[step - 1, 1:2, :] - spans_all[step - 1, 0:1, :]).astype(F32)
            span_sum = span_sum + jnp.where(live, lengths, 0.0)
            table = narr_all[step - 1]
        else:
            live, table = own_live, narr_ref[...]
        narrs.append(table)
        scores = logit_scale * contracted_columns(embedded, table)
        if step == 0:
            own_scores = scores
        masked.append(jnp.where(live, scores, -jnp.inf))
    label_total = jnp.sum(span_sum, axis=1, keepdims=True)
    highest = functools.reduce(jnp.maximum, [jnp.max(m, axis=1, keepdims=True) for m in masked])
    powers = [jnp.exp(m - highest) for m in masked]
    total = functools.reduce(jnp.add, [jnp.sum(e, axis=1, keepdims=True) for e in powers])
    log_total = highest + jnp.log(total)
    local_loss = jnp.sum(labeled * log_total, axis=0, keepdims=True) - jnp.sum(
        jnp.sum(member * own_scores, axis=1, keepdims=True), axis=0, keepdims=True
    )
    factor = (length * n * videos) / label_total
    weight = labeled / total
    embed_sum = None
    for step in range(videos):
        probs = powers[step] * weight
        if step == 0:
            probs = probs - member
        term = jnp.dot((probs * factor).astype(BF16), narrs[step], preferred_element_type=F32)
        embed_sum = term if embed_sum is None else embed_sum + term
    embed_grad = (logit_scale * embed_sum).astype(BF16)
    out_grad[...] = contracted_columns(embed_grad, head_ref[...]).astype(BF16)
    pre[...] = jnp.where(hidden[...] > 0.0, out_grad[...].astype(F32), 0.0).astype(BF16)
    pl.when(has_next)(pre_up.start)
    pl.when(has_prev)(pre_down.start)

    taps = (earlier, frames_ref.at[0], later)
    slabs = [buffers[13 * p:13 * (p + 1)] for p in range(len(parts))]
    band = slabs[0][0].shape[-2]

    def scatter(values, slab, first):
        accum, sent0 = slab[0], slab[1]
        width = values.shape[1]
        for z in range(runs):
            for x in range(2):
                for y in range(2):
                    for c in range(2):
                        at = (((z * 2 + x) * 2 + y) * 2 + c) * band
                        accum[c, y, x, z, :, first:first + width] = values[at:at + band]

    def send_first(slab):
        accum, sent0, recv0 = slab[0], slab[1], slab[2]
        sent0[...] = accum[1 - core].astype(BF16)
        copy = remote(sent0, recv0, slab[9].at[0], slab[10].at[0], across_core)
        copy.start()
        return copy

    first_copies = []
    for (pieces, order), slab in zip(parts, slabs):
        first = 0
        for tap, low, high in pieces:
            if tap == 3:
                values = contracted_rows(layer_out, embed_grad[:, low:high])
            else:
                values = contracted_rows(taps[tap][...], pre[:, low:high])
            scatter(values, slab, first)
            first += high - low
        first_copies.append(send_first(slab))

    bias_local = jnp.sum(pre[...].astype(F32), axis=0, keepdims=True)
    rows = lax.broadcasted_iota(jnp.int32, small_ref.shape, 0)
    small = jnp.where(rows == 0, bias_local, jnp.where(rows == 1, local_loss, 0.0))
    small_copies = []

    def small_start(index, peers_of):
        started = []
        for k, peer in enumerate(peers_of):
            copy = remote(small_send.at[index], small_recv.at[index + k], small_ssem.at[index + k], small_rsem.at[index + k], peer)
            copy.start()
            started.append(copy)
        small_copies.extend(started)
        return started

    small_send[0] = small
    small_now = small_start(0, [across_core])

    second_copies = []
    for (pieces, order), slab, copy in zip(parts, slabs, first_copies):
        accum, recv0, sent1, recv1 = slab[0], slab[2], slab[3], slab[4]
        copy.wait_recv()
        if order == "rows":
            for x in range(2):
                sent1[x] = (accum[core, 1 - row, x] + recv0[1 - row, x].astype(F32)).astype(BF16)
            peer = across_row
        else:
            for y in range(2):
                sent1[y] = (accum[core, y, 1 - side] + recv0[y, 1 - side].astype(F32)).astype(BF16)
            peer = across_side
        copy = remote(sent1, recv1, slab[9].at[1], slab[10].at[1], peer)
        copy.start()
        second_copies.append(copy)
    small_now[0].wait_recv()
    small = small + small_recv[0]
    small_send[1] = small
    small_now = small_start(1, [across_row])

    grad = out_grad[...].astype(F32) + contracted_columns(pre[...], weight_ref[1])
    pl.when(has_prev)(pre_up.wait_recv)
    grad = grad + contracted_columns(pre_prev[...], weight_ref[2])
    pl.when(has_next)(pre_down.wait_recv)
    grad = grad + contracted_columns(pre_next[...], weight_ref[0])
    input_ref[0] = grad.astype(BF16)

    third_copies = []
    for (pieces, order), slab, copy in zip(parts, slabs, second_copies):
        accum, recv0, recv1, sent2, recv2 = slab[0], slab[2], slab[4], slab[5], slab[6]
        copy.wait_recv()
        if order == "rows":
            sent2[...] = (accum[core, row, 1 - side] + recv0[row, 1 - side].astype(F32) + recv1[1 - side].astype(F32)).astype(BF16)
            peer = across_side
        else:
            sent2[...] = (accum[core, 1 - row, side] + recv0[1 - row, side].astype(F32) + recv1[1 - row].astype(F32)).astype(BF16)
            peer = across_row
        copy = remote(sent2, recv2, slab[9].at[2], slab[10].at[2], peer)
        copy.start()
        third_copies.append(copy)
    small_now[0].wait_recv()
    small = small + small_recv[1]
    small_send[2] = small
    small_now = small_start(2, [across_side])

    run_copies = []
    for (pieces, order), slab, copy in zip(parts, slabs, third_copies):
        accum, recv0, recv1, recv2, sent3, recv3 = slab[0], slab[2], slab[4], slab[6], slab[7], slab[8]
        copy.wait_recv()
        kept = recv1.at[side] if order == "rows" else recv1.at[row]
        started = []
        for step in range(1, runs):
            z = lax.rem(deep + step, runs)
            sent3[step] = (
                accum[core, row, side, z] + recv0[row, side, z].astype(F32) + kept[z].astype(F32) + recv2[z].astype(F32)
            ).astype(BF16)
            copy = remote(sent3.at[step], recv3.at[step], slab[9].at[2 + step], slab[10].at[2 + step], at_run(step))
            copy.start()
            started.append(copy)
        run_copies.append(started)
    small_now[0].wait_recv()
    small = small + small_recv[2]
    small_send[3] = small
    small_now = small_start(3, [at_run(s) for s in range(1, runs)])

    final_copies = []
    for (pieces, order), slab, started in zip(parts, slabs, run_copies):
        accum, recv0, recv1, recv2, recv3 = slab[0], slab[2], slab[4], slab[6], slab[8]
        final, fsend, frecv = slab[11], slab[9], slab[10]
        final_in = slab[12]
        kept = recv1.at[side] if order == "rows" else recv1.at[row]
        value = accum[core, row, side, deep] + recv0[row, side, deep].astype(F32) + kept[deep].astype(F32) + recv2[deep].astype(F32)
        for step in range(1, runs):
            started[step - 1].wait_recv()
            value = value + recv3[step].astype(F32)
        final[...] = value.astype(BF16)
        copies = []
        for step in range(1, videos):
            index = 1 + runs + step
            copy = remote(final, final_in.at[step - 1], fsend.at[index], frecv.at[index], at_video(step))
            copy.start()
            copies.append(copy)
        final_copies.append(copies)

    for copy in small_now:
        copy.wait_recv()
    total_small = None
    for z in range(runs):
        step = lax.rem(deep - z + runs, runs)
        term = small
        for s in range(1, runs):
            term = jnp.where(step == s, small_recv[2 + s], term)
        total_small = term if total_small is None else total_small + term
    rows = lax.broadcasted_iota(jnp.int32, small_ref.shape, 0)
    small_ref[...] = jnp.where(rows == 1, total_small / label_total, total_small)

    for (pieces, order), slab, copies in zip(parts, slabs, final_copies):
        for step in range(videos):
            if step:
                copies[step - 1].wait_recv()
                value = slab[12][step - 1]
            else:
                value = slab[11][...]
            value = value.astype(F32)
            at = pl.ds(pl.multiple_of(lax.rem(vid + videos - step, videos) * band, band), band)
            first = 0
            for tap, low, high in pieces:
                piece = value[:, first:first + high - low]
                if tap == 3:
                    head_out_ref[at, low:high] = piece
                else:
                    dil_ref[tap, at, low:high] = piece
                first += high - low

    pl.when(has_next)(frames_up.wait_send)
    pl.when(has_prev)(frames_down.wait_send)
    pl.when(has_next)(pre_up.wait_send)
    pl.when(has_prev)(pre_down.wait_send)
    for copy in gathers + first_copies + small_copies + second_copies + third_copies:
        copy.wait_send()
    for started in run_copies + final_copies:
        for copy in started:
            copy.wait_send()


def section(n, videos, frames, dilated_weight, dilated_bias, head_matrix, narrations, narration_counts, narration_spans):
    length, channels = frames.shape[1:]
    width, slots = head_matrix.shape[1], narrations.shape[0]
    rows, runs = channels // n, n // 2
    band = rows // videos
    half, head_half = channels // 2, width // 2
    parts = tuple(
        (tuple((tap, p * half, (p + 1) * half) for tap in range(3)) + ((3, p * head_half, (p + 1) * head_half),), order)
        for p, order in enumerate(("rows", "sides"))
    )
    scratch = [
        pltpu.VMEM((length, channels), BF16),
        pltpu.VMEM((length, channels), BF16),
        pltpu.VMEM((videos - 1, slots, width), BF16),
        pltpu.VMEM((videos - 1, 2, slots), jnp.int32),
        pltpu.VMEM((length, channels), F32),
        pltpu.VMEM((length, channels), BF16),
        pltpu.VMEM((length, channels), BF16),
        pltpu.VMEM((length, channels), BF16),
        pltpu.VMEM((length, channels), BF16),
        pltpu.VMEM((4, 8, channels), F32),
        pltpu.VMEM((2 + runs, 8, channels), F32),
        pltpu.SemaphoreType.DMA((4,)),
        pltpu.SemaphoreType.DMA((4,)),
        pltpu.SemaphoreType.DMA((2, videos - 1)),
        pltpu.SemaphoreType.DMA((2, videos - 1)),
        pltpu.SemaphoreType.DMA((2 + runs,)),
        pltpu.SemaphoreType.DMA((2 + runs,)),
    ]
    for pieces, order in parts:
        columns = sum(high - low for _, low, high in pieces)
        scratch += [
            pltpu.VMEM((2, 2, 2, runs, band, columns), F32),
            pltpu.VMEM((2, 2, runs, band, columns), BF16),
            pltpu.VMEM((2, 2, runs, band, columns), BF16),
            pltpu.VMEM((2, runs, band, columns), BF16),
            pltpu.VMEM((2, runs, band, columns), BF16),
            pltpu.VMEM((runs, band, columns), BF16),
            pltpu.VMEM((runs, band, columns), BF16),
            pltpu.VMEM((runs, band, columns), BF16),
            pltpu.VMEM((runs, band, columns), BF16),
            pltpu.SemaphoreType.DMA((1 + runs + videos,)),
            pltpu.SemaphoreType.DMA((1 + runs + videos,)),
            pltpu.VMEM((band, columns), BF16),
            pltpu.VMEM((videos - 1, band, columns), BF16),
        ]
    vmem = pl.BlockSpec(memory_space=pltpu.VMEM)
    dil, head, inputs, small = pl.pallas_call(
        functools.partial(section_kernel, n, videos, parts),
        out_shape=(
            jax.ShapeDtypeStruct((3, rows, channels), F32),
            jax.ShapeDtypeStruct((rows, width), F32),
            jax.ShapeDtypeStruct((1, length, channels), BF16),
            jax.ShapeDtypeStruct((8, channels), F32),
        ),
        in_specs=[pl.BlockSpec(memory_space=pltpu.SMEM)] + [vmem] * 6,
        out_specs=(vmem,) * 4,
        scratch_shapes=scratch,
        compiler_params=pltpu.CompilerParams(
            collective_id=0, has_side_effects=True, vmem_limit_bytes=48 * 1024 * 1024
        ),
    )(
        narration_counts, frames, dilated_weight, dilated_bias[None], head_matrix, narrations,
        narration_spans[0].T,
    )
    return small[1, 0], dil, head, small[0], inputs


def solution(mesh):
    n, videos = mesh.shape["tm"], mesh.shape["video"]

    def body(*arrays):
        frames, weight = arrays[0], arrays[1]
        if videos == 4 and n % 4 == 0 and weight.shape[1] % (16 * n * videos) == 0:
            return section(n, videos, *arrays)
        return per_device(*arrays)

    return jax.shard_map(
        body,
        mesh=mesh,
        in_specs=(
            P("video", "tm", None),
            P(),
            P(),
            P(),
            P("video", None),
            P(),
            P("video", None, None),
        ),
        out_specs=(P(), P(None, "tm", None), P("tm", None), P(), P("video", "tm", None)),
        check_vma=False,
    )
```

```python
import functools

import jax
import jax.numpy as jnp
from jax import lax
from jax.experimental import pallas as pl
from jax.experimental.pallas import tpu as pltpu
from jax.sharding import PartitionSpec as P

SHIFT_N = 2


logit_scale = 0.0625


def passed_along(value, axis, steps):
    count = lax.axis_size(axis)
    first, last = (max(0, -steps), min(count, count - steps))
    return lax.ppermute(value, axis, [(source, source + steps) for source in range(first, last)])


def moved(values, offset):
    return passed_along(values, "tm", offset)


def moved_back(values, offset):
    return passed_along(values, "tm", offset)


def contracted_rows(left, right):
    return lax.dot_general(
        left, right, (((0,), (0,)), ((), ())), preferred_element_type=jnp.float32
    )


def contracted_columns(left, right):
    return lax.dot_general(
        left, right, (((1,), (1,)), ((), ())), preferred_element_type=jnp.float32
    )


def per_device(
    frames, dilated_weight, dilated_bias, head_matrix, narrations, narration_counts, narration_spans
):
    present_tap = frames[0]
    length = present_tap.shape[0]
    narr_local = narrations.shape[0]
    preceding_tap = moved(present_tap, SHIFT_N)
    following_tap = moved(present_tap, -SHIFT_N)
    middle_frames = jnp.dot(present_tap, dilated_weight[1], preferred_element_type=jnp.float32)
    hidden_state = (
        middle_frames
        + jnp.dot(preceding_tap, dilated_weight[0], preferred_element_type=jnp.float32)
        + jnp.dot(following_tap, dilated_weight[2], preferred_element_type=jnp.float32)
        + dilated_bias
    )
    layer_out = (present_tap.astype(jnp.float32) + jnp.maximum(hidden_state, 0.0)).astype(
        jnp.bfloat16
    )
    embedded = jnp.dot(layer_out, head_matrix, preferred_element_type=jnp.float32).astype(
        jnp.bfloat16
    )
    every_narr = lax.all_gather(narrations, "video", axis=0, tiled=True)
    scores = logit_scale * contracted_columns(embedded, every_narr)
    slots = jnp.arange(narr_local, dtype=jnp.int32)
    valid = (slots[None, :] < narration_counts[:, None]).reshape(-1)
    masked = jnp.where(valid[None, :], scores, -jnp.inf)
    highest = jnp.max(masked, axis=1, keepdims=True)
    log_total = highest + jnp.log(jnp.sum(jnp.exp(masked - highest), axis=1, keepdims=True))
    video_index = lax.axis_index("video")
    own_count = lax.dynamic_index_in_dim(narration_counts, video_index, 0, keepdims=False)
    spans = narration_spans[0]
    positions = lax.axis_index("tm") * length + jnp.arange(length, dtype=jnp.int32)
    member = (
        (positions[:, None] >= spans[None, :, 0])
        & (positions[:, None] < spans[None, :, 1])
        & (slots[None, :] < own_count)
    ).astype(jnp.float32)
    labeled = jnp.sum(member, axis=1)
    own_start = video_index * narr_local
    own_scores = lax.dynamic_slice_in_dim(scores, own_start, narr_local, 1)
    local_loss = jnp.sum(labeled * log_total[:, 0]) - jnp.sum(member * own_scores)
    span_lengths = jnp.where(slots < own_count, spans[:, 1] - spans[:, 0], 0).astype(jnp.float32)
    label_total = lax.psum(jnp.sum(span_lengths), "video")
    factor = length * lax.axis_size("tm") * lax.axis_size("video") / label_total
    probs = jnp.exp(masked - log_total) * labeled[:, None]
    own_grad = lax.dynamic_slice_in_dim(probs, own_start, narr_local, 1) - member
    score_grad = lax.dynamic_update_slice_in_dim(probs, own_grad, own_start, 1)
    score_grad = (score_grad * factor).astype(jnp.bfloat16)
    embed_grad = (
        logit_scale * jnp.dot(score_grad, every_narr, preferred_element_type=jnp.float32)
    ).astype(jnp.bfloat16)
    head_resident = contracted_rows(layer_out, embed_grad)
    output_gradient = contracted_columns(embed_grad, head_matrix).astype(jnp.bfloat16)
    preactivation_gradient = jnp.where(
        hidden_state > 0.0, output_gradient.astype(jnp.float32), 0.0
    ).astype(jnp.bfloat16)
    received_following = moved_back(preactivation_gradient, -SHIFT_N)
    received_preceding = moved_back(preactivation_gradient, SHIFT_N)
    bias_local = jnp.sum(preactivation_gradient.astype(jnp.float32), axis=0)
    dilated_resident = jnp.stack(
        [
            contracted_rows(preceding_tap, preactivation_gradient),
            contracted_rows(present_tap, preactivation_gradient),
            contracted_rows(following_tap, preactivation_gradient),
        ]
    )
    input_gradient = (
        output_gradient.astype(jnp.float32)
        + contracted_columns(preactivation_gradient, dilated_weight[1])
        + contracted_columns(received_following, dilated_weight[0])
        + contracted_columns(received_preceding, dilated_weight[2])
    )
    loss_total, bias_overall = lax.psum((local_loss, bias_local), ("tm", "video"))
    dilated_complete, head_complete = lax.psum((dilated_resident, head_resident), "video")
    dilated_fraction, head_fraction = (
        lax.psum_scatter(dilated_complete, "tm", scatter_dimension=1, tiled=True),
        lax.psum_scatter(head_complete[None], "tm", scatter_dimension=1, tiled=True),
    )
    loss = loss_total / label_total
    return (
        loss,
        dilated_fraction,
        head_fraction[0],
        bias_overall,
        input_gradient.astype(jnp.bfloat16)[None],
    )


MESH = pl.DeviceIdType.MESH
F32, BF16 = jnp.float32, jnp.bfloat16


def section_kernel(
    n, videos, parts,
    counts_hbm, frames_hbm, weight_hbm, bias_hbm, head_hbm, narr_hbm, spans_hbm,
    dil_ref, head_out_ref, input_ref, bias_out_ref, loss_ref,
    counts_ref, frames_ref, weight_ref, bias_ref, head_ref, narr_ref, spans_ref, load_sem, turned,
    earlier, later, narr_all, spans_all, hidden, out_grad, pre, pre_next, pre_prev,
    small_send, small_recv, edge_send, edge_recv, gather_send, gather_recv,
    small_ssem, small_rsem, *buffers,
):
    loads = [
        pltpu.make_async_copy(source, target, load_sem.at[k])
        for k, (source, target) in enumerate(
            (
                (frames_hbm, frames_ref), (weight_hbm, weight_ref), (bias_hbm, bias_ref), (spans_hbm, spans_ref),
                (counts_hbm, counts_ref), (head_hbm, head_ref), (narr_hbm, narr_ref),
            )
        )
    ]
    for copy in loads:
        copy.start()
    tm, vid = lax.axis_index("tm"), lax.axis_index("video")
    runs = n // 2
    core, row = lax.rem(vid, 2), lax.div(vid, 2)
    side, deep = lax.rem(tm, 2), lax.div(tm, 2)
    across_core = {"tm": tm, "video": vid + 1 - 2 * core}
    across_row = {"tm": tm, "video": lax.rem(vid + 2, videos)}
    across_side = {"tm": tm + 1 - 2 * side, "video": vid}

    def at_run(step):
        return {"tm": lax.rem(tm + 2 * step, n), "video": vid}

    def at_video(step):
        return {"tm": tm, "video": lax.rem(vid + step, videos)}

    barrier = pltpu.get_barrier_semaphore()
    peers = [across_side] + [at_run(s) for s in range(1, runs)] + [at_video(s) for s in range(1, videos)]
    for peer in peers:
        pl.semaphore_signal(barrier, inc=1, device_id=peer, device_id_type=MESH)
    pl.semaphore_wait(barrier, len(peers))

    def remote(src, dst, ssem, rsem, peer):
        return pltpu.make_async_remote_copy(
            src_ref=src, dst_ref=dst, send_sem=ssem, recv_sem=rsem, device_id=peer, device_id_type=MESH
        )

    has_prev, has_next = tm >= SHIFT_N, tm < n - SHIFT_N
    up = {"tm": lax.rem(tm + SHIFT_N, n), "video": vid}
    down = {"tm": lax.rem(tm + n - SHIFT_N, n), "video": vid}
    frames_up = remote(frames_hbm.at[0], earlier, edge_send.at[0], edge_recv.at[0], up)
    frames_down = remote(frames_hbm.at[0], later, edge_send.at[1], edge_recv.at[1], down)
    pre_up = remote(pre, pre_prev, edge_send.at[2], edge_recv.at[2], up)
    pre_down = remote(pre, pre_next, edge_send.at[3], edge_recv.at[3], down)
    pl.when(has_next)(frames_up.start)
    pl.when(has_prev)(frames_down.start)
    gathers = []
    for step in range(1, videos):
        gathers.append(remote(spans_hbm, spans_all.at[step - 1], gather_send.at[0, step - 1], gather_recv.at[0, step - 1], at_video(step)))
        gathers.append(remote(narr_hbm, narr_all.at[step - 1], gather_send.at[1, step - 1], gather_recv.at[1, step - 1], at_video(step)))
    for copy in gathers:
        copy.start()

    def no_prev():
        earlier[...] = jnp.zeros_like(earlier)
        pre_prev[...] = jnp.zeros_like(pre_prev)

    def no_next():
        later[...] = jnp.zeros_like(later)
        pre_next[...] = jnp.zeros_like(pre_next)

    pl.when(jnp.logical_not(has_prev))(no_prev)
    pl.when(jnp.logical_not(has_next))(no_next)

    for copy in loads:
        copy.wait()
    present = frames_ref[0]
    turned[...] = present.T
    length = present.shape[0]
    slots_count = narr_ref.shape[0]
    hidden[...] = jnp.dot(present, weight_ref[1], preferred_element_type=F32) + bias_ref[...]
    slots = lax.broadcasted_iota(jnp.int32, (1, slots_count), 1)
    positions = tm * length + lax.broadcasted_iota(jnp.int32, (length, 1), 0)
    starts, ends = spans_ref[0:1, :], spans_ref[1:2, :]
    own_live = slots < counts_ref[vid]
    member = ((positions >= starts) & (positions < ends) & own_live).astype(F32)
    labeled = jnp.sum(member, axis=1, keepdims=True)

    def recv_up():
        frames_up.wait_recv()

    pl.when(has_prev)(recv_up)
    hidden[...] += jnp.dot(earlier[...], weight_ref[0], preferred_element_type=F32)
    pl.when(has_next)(frames_down.wait_recv)
    hidden[...] += jnp.dot(later[...], weight_ref[2], preferred_element_type=F32)
    layer_out = (present.astype(F32) + jnp.maximum(hidden[...], 0.0)).astype(BF16)
    embedded = jnp.dot(layer_out, head_ref[...], preferred_element_type=F32).astype(BF16)

    span_sum = jnp.where(own_live, (ends - starts).astype(F32), 0.0)
    narrs, masked = [], []
    for step in range(videos):
        if step:
            gathers[2 * (step - 1)].wait_recv()
            gathers[2 * (step - 1) + 1].wait_recv()
            live = slots < counts_ref[lax.rem(vid + videos - step, videos)]
            lengths = (spans_all[step - 1, 1:2, :] - spans_all[step - 1, 0:1, :]).astype(F32)
            span_sum = span_sum + jnp.where(live, lengths, 0.0)
            table = narr_all[step - 1]
        else:
            live, table = own_live, narr_ref[...]
        narrs.append(table)
        scores = logit_scale * contracted_columns(embedded, table)
        if step == 0:
            own_scores = scores
        masked.append(jnp.where(live, scores, -jnp.inf))
    label_total = jnp.sum(span_sum, axis=1, keepdims=True)
    highest = functools.reduce(jnp.maximum, [jnp.max(m, axis=1, keepdims=True) for m in masked])
    powers = [jnp.exp(m - highest) for m in masked]
    total = functools.reduce(jnp.add, [jnp.sum(e, axis=1, keepdims=True) for e in powers])
    log_total = highest + jnp.log(total)
    local_loss = jnp.sum(labeled * log_total, axis=0, keepdims=True) - jnp.sum(
        jnp.sum(member * own_scores, axis=1, keepdims=True), axis=0, keepdims=True
    )
    factor = (length * n * videos) / label_total
    weight = labeled / total
    embed_sum = None
    for step in range(videos):
        probs = powers[step] * weight
        if step == 0:
            probs = probs - member
        term = jnp.dot((probs * factor).astype(BF16), narrs[step], preferred_element_type=F32)
        embed_sum = term if embed_sum is None else embed_sum + term
    embed_grad = (logit_scale * embed_sum).astype(BF16)
    out_grad[...] = contracted_columns(embed_grad, head_ref[...]).astype(BF16)
    pre[...] = jnp.where(hidden[...] > 0.0, out_grad[...].astype(F32), 0.0).astype(BF16)
    pl.when(has_next)(pre_up.start)
    pl.when(has_prev)(pre_down.start)

    taps = (earlier, frames_ref.at[0], later)
    slabs = [buffers[13 * p:13 * (p + 1)] for p in range(len(parts))]
    band = slabs[0][0].shape[-2]

    def scatter(values, slab, first):
        accum, sent0 = slab[0], slab[1]
        width = values.shape[1]
        for z in range(runs):
            for x in range(2):
                for y in range(2):
                    for c in range(2):
                        at = (((z * 2 + x) * 2 + y) * 2 + c) * band
                        accum[c, y, x, z, :, first:first + width] = values[at:at + band]

    def send_first(slab):
        accum, sent0, recv0 = slab[0], slab[1], slab[2]
        sent0[...] = accum[1 - core].astype(BF16)
        copy = remote(sent0, recv0, slab[9].at[0], slab[10].at[0], across_core)
        copy.start()
        return copy

    first_copies = []
    for (pieces, order), slab in zip(parts, slabs):
        first = 0
        for tap, low, high in pieces:
            if tap == 3:
                values = contracted_rows(layer_out, embed_grad[:, low:high])
            elif tap == 1:
                values = jnp.dot(turned[...], pre[:, low:high], preferred_element_type=F32)
            else:
                values = contracted_rows(taps[tap][...], pre[:, low:high])
            scatter(values, slab, first)
            first += high - low
        first_copies.append(send_first(slab))

    bias_local = jnp.sum(pre[...].astype(F32), axis=0, keepdims=True)
    rows = lax.broadcasted_iota(jnp.int32, small_send.shape[1:], 0)
    small = jnp.where(rows == 0, bias_local, jnp.where(rows == 1, local_loss, 0.0))
    small_copies = []

    def small_start(index, peers_of):
        started = []
        for k, peer in enumerate(peers_of):
            copy = remote(small_send.at[index], small_recv.at[index + k], small_ssem.at[index + k], small_rsem.at[index + k], peer)
            copy.start()
            started.append(copy)
        small_copies.extend(started)
        return started

    small_send[0] = small
    small_now = small_start(0, [across_core])

    second_copies = []
    for (pieces, order), slab, copy in zip(parts, slabs, first_copies):
        accum, recv0, sent1, recv1 = slab[0], slab[2], slab[3], slab[4]
        copy.wait_recv()
        if order == "rows":
            for x in range(2):
                sent1[x] = (accum[core, 1 - row, x] + recv0[1 - row, x].astype(F32)).astype(BF16)
            peer = across_row
        else:
            for y in range(2):
                sent1[y] = (accum[core, y, 1 - side] + recv0[y, 1 - side].astype(F32)).astype(BF16)
            peer = across_side
        copy = remote(sent1, recv1, slab[9].at[1], slab[10].at[1], peer)
        copy.start()
        second_copies.append(copy)
    small_now[0].wait_recv()
    small = small + small_recv[0]
    small_send[1] = small
    small_now = small_start(1, [across_row])

    grad = out_grad[...].astype(F32) + contracted_columns(pre[...], weight_ref[1])
    pl.when(has_prev)(pre_up.wait_recv)
    grad = grad + contracted_columns(pre_prev[...], weight_ref[2])
    pl.when(has_next)(pre_down.wait_recv)
    grad = grad + contracted_columns(pre_next[...], weight_ref[0])
    input_ref[0] = grad.astype(BF16)

    third_copies = []
    for (pieces, order), slab, copy in zip(parts, slabs, second_copies):
        accum, recv0, recv1, sent2, recv2 = slab[0], slab[2], slab[4], slab[5], slab[6]
        copy.wait_recv()
        if order == "rows":
            sent2[...] = (accum[core, row, 1 - side] + recv0[row, 1 - side].astype(F32) + recv1[1 - side].astype(F32)).astype(BF16)
            peer = across_side
        else:
            sent2[...] = (accum[core, 1 - row, side] + recv0[1 - row, side].astype(F32) + recv1[1 - row].astype(F32)).astype(BF16)
            peer = across_row
        copy = remote(sent2, recv2, slab[9].at[2], slab[10].at[2], peer)
        copy.start()
        third_copies.append(copy)
    small_now[0].wait_recv()
    small = small + small_recv[1]
    small_send[2] = small
    small_now = small_start(2, [across_side])

    run_copies = []
    for (pieces, order), slab, copy in zip(parts, slabs, third_copies):
        accum, recv0, recv1, recv2, sent3, recv3 = slab[0], slab[2], slab[4], slab[6], slab[7], slab[8]
        copy.wait_recv()
        kept = recv1.at[side] if order == "rows" else recv1.at[row]
        started = []
        for step in range(1, runs):
            z = lax.rem(deep + step, runs)
            sent3[step] = (
                accum[core, row, side, z] + recv0[row, side, z].astype(F32) + kept[z].astype(F32) + recv2[z].astype(F32)
            ).astype(BF16)
            copy = remote(sent3.at[step], recv3.at[step], slab[9].at[2 + step], slab[10].at[2 + step], at_run(step))
            copy.start()
            started.append(copy)
        run_copies.append(started)
    small_now[0].wait_recv()
    small = small + small_recv[2]
    small_send[3] = small
    small_now = small_start(3, [at_run(s) for s in range(1, runs)])

    final_copies = []
    for (pieces, order), slab, started in zip(parts, slabs, run_copies):
        accum, recv0, recv1, recv2, recv3 = slab[0], slab[2], slab[4], slab[6], slab[8]
        final, fsend, frecv = slab[11], slab[9], slab[10]
        final_in = slab[12]
        kept = recv1.at[side] if order == "rows" else recv1.at[row]
        value = accum[core, row, side, deep] + recv0[row, side, deep].astype(F32) + kept[deep].astype(F32) + recv2[deep].astype(F32)
        for step in range(1, runs):
            started[step - 1].wait_recv()
            value = value + recv3[step].astype(F32)
        final[...] = value.astype(BF16)
        copies = []
        for step in range(1, videos):
            index = 1 + runs + step
            copy = remote(final, final_in.at[step - 1], fsend.at[index], frecv.at[index], at_video(step))
            copy.start()
            copies.append(copy)
        final_copies.append(copies)

    for copy in small_now:
        copy.wait_recv()
    total_small = None
    for z in range(runs):
        step = lax.rem(deep - z + runs, runs)
        term = small
        for s in range(1, runs):
            term = jnp.where(step == s, small_recv[2 + s], term)
        total_small = term if total_small is None else total_small + term
    bias_out_ref[...] = total_small[0:1]
    loss_ref[...] = total_small[1:2, 0:1] / label_total

    for (pieces, order), slab, copies in zip(parts, slabs, final_copies):
        for step in range(videos):
            if step:
                copies[step - 1].wait_recv()
                value = slab[12][step - 1]
            else:
                value = slab[11][...]
            value = value.astype(F32)
            at = pl.ds(pl.multiple_of(lax.rem(vid + videos - step, videos) * band, band), band)
            first = 0
            for tap, low, high in pieces:
                piece = value[:, first:first + high - low]
                if tap == 3:
                    head_out_ref[at, low:high] = piece
                else:
                    dil_ref[tap, at, low:high] = piece
                first += high - low

    pl.when(has_next)(frames_up.wait_send)
    pl.when(has_prev)(frames_down.wait_send)
    pl.when(has_next)(pre_up.wait_send)
    pl.when(has_prev)(pre_down.wait_send)
    for copy in gathers + first_copies + small_copies + second_copies + third_copies:
        copy.wait_send()
    for started in run_copies + final_copies:
        for copy in started:
            copy.wait_send()


def write_kernel(*refs):
    sems = refs[10]
    copies = [pltpu.make_async_copy(refs[k], refs[5 + k], sems.at[k]) for k in range(5)]
    for copy in copies:
        copy.start()
    for copy in copies:
        copy.wait()


def section(n, videos, frames, dilated_weight, dilated_bias, head_matrix, narrations, narration_counts, narration_spans):
    length, channels = frames.shape[1:]
    width, slots = head_matrix.shape[1], narrations.shape[0]
    rows, runs = channels // n, n // 2
    band = rows // videos
    half, head_half = channels // 2, width // 2
    parts = (
        (((1, 0, channels),), "rows"),
        (((0, 0, channels),), "sides"),
        (((2, 0, half), (3, 0, head_half)), "rows"),
        (((2, half, channels), (3, head_half, width)), "sides"),
    )
    scratch = [
        pltpu.SMEM((videos,), jnp.int32),
        pltpu.VMEM((1, length, channels), BF16),
        pltpu.VMEM((3, channels, channels), BF16),
        pltpu.VMEM((1, channels), F32),
        pltpu.VMEM((channels, width), BF16),
        pltpu.VMEM((slots, width), BF16),
        pltpu.VMEM((2, slots), jnp.int32),
        pltpu.SemaphoreType.DMA((7,)),
        pltpu.VMEM((channels, length), BF16),
        pltpu.VMEM((length, channels), BF16),
        pltpu.VMEM((length, channels), BF16),
        pltpu.VMEM((videos - 1, slots, width), BF16),
        pltpu.VMEM((videos - 1, 2, slots), jnp.int32),
        pltpu.VMEM((length, channels), F32),
        pltpu.VMEM((length, channels), BF16),
        pltpu.VMEM((length, channels), BF16),
        pltpu.VMEM((length, channels), BF16),
        pltpu.VMEM((length, channels), BF16),
        pltpu.VMEM((4, 8, channels), F32),
        pltpu.VMEM((2 + runs, 8, channels), F32),
        pltpu.SemaphoreType.DMA((4,)),
        pltpu.SemaphoreType.DMA((4,)),
        pltpu.SemaphoreType.DMA((2, videos - 1)),
        pltpu.SemaphoreType.DMA((2, videos - 1)),
        pltpu.SemaphoreType.DMA((2 + runs,)),
        pltpu.SemaphoreType.DMA((2 + runs,)),
    ]
    for pieces, order in parts:
        columns = sum(high - low for _, low, high in pieces)
        scratch += [
            pltpu.VMEM((2, 2, 2, runs, band, columns), F32),
            pltpu.VMEM((2, 2, runs, band, columns), BF16),
            pltpu.VMEM((2, 2, runs, band, columns), BF16),
            pltpu.VMEM((2, runs, band, columns), BF16),
            pltpu.VMEM((2, runs, band, columns), BF16),
            pltpu.VMEM((runs, band, columns), BF16),
            pltpu.VMEM((runs, band, columns), BF16),
            pltpu.VMEM((runs, band, columns), BF16),
            pltpu.VMEM((runs, band, columns), BF16),
            pltpu.SemaphoreType.DMA((1 + runs + videos,)),
            pltpu.SemaphoreType.DMA((1 + runs + videos,)),
            pltpu.VMEM((band, columns), BF16),
            pltpu.VMEM((videos - 1, band, columns), BF16),
        ]
    vmem, hbm = pl.BlockSpec(memory_space=pltpu.VMEM), pl.BlockSpec(memory_space=pltpu.HBM)
    shapes = (
        jax.ShapeDtypeStruct((3, rows, channels), F32),
        jax.ShapeDtypeStruct((rows, width), F32),
        jax.ShapeDtypeStruct((1, length, channels), BF16),
        jax.ShapeDtypeStruct((1, channels), F32),
        jax.ShapeDtypeStruct((1, 1), F32),
    )
    results = pl.pallas_call(
        functools.partial(section_kernel, n, videos, parts),
        out_shape=shapes,
        in_specs=[hbm] * 7,
        out_specs=(vmem,) * 5,
        scratch_shapes=scratch,
        compiler_params=pltpu.CompilerParams(
            collective_id=0, has_side_effects=True, vmem_limit_bytes=48 * 1024 * 1024
        ),
    )(
        *(
            pltpu.with_memory_space_constraint(array, pltpu.HBM)
            for array in (
                narration_counts, frames, dilated_weight, dilated_bias[None], head_matrix, narrations,
                narration_spans[0].T,
            )
        )
    )
    dil, head, inputs, bias, loss = pl.pallas_call(
        write_kernel,
        out_shape=shapes,
        in_specs=[vmem] * 5,
        out_specs=(hbm,) * 5,
        scratch_shapes=[pltpu.SemaphoreType.DMA((5,))],
        compiler_params=pltpu.CompilerParams(vmem_limit_bytes=1024 * 1024),
    )(*results)
    return loss[0, 0], dil, head, bias[0], inputs


def solution(mesh):
    n, videos = mesh.shape["tm"], mesh.shape["video"]

    def body(*arrays):
        frames, weight = arrays[0], arrays[1]
        if videos == 4 and n % 4 == 0 and weight.shape[1] % (16 * n * videos) == 0:
            return section(n, videos, *arrays)
        return per_device(*arrays)

    return jax.shard_map(
        body,
        mesh=mesh,
        in_specs=(
            P("video", "tm", None),
            P(),
            P(),
            P(),
            P("video", None),
            P(),
            P("video", None, None),
        ),
        out_specs=(P(), P(None, "tm", None), P("tm", None), P(), P("video", "tm", None)),
        check_vma=False,
    )
```

```python
import functools

import jax
import jax.numpy as jnp
from jax import lax
from jax.experimental import pallas as pl
from jax.experimental.pallas import tpu as pltpu
from jax.sharding import PartitionSpec as P

SHIFT_N = 2


logit_scale = 0.0625


def passed_along(value, axis, steps):
    count = lax.axis_size(axis)
    first, last = (max(0, -steps), min(count, count - steps))
    return lax.ppermute(value, axis, [(source, source + steps) for source in range(first, last)])


def moved(values, offset):
    return passed_along(values, "tm", offset)


def moved_back(values, offset):
    return passed_along(values, "tm", offset)


def contracted_rows(left, right):
    return lax.dot_general(
        left, right, (((0,), (0,)), ((), ())), preferred_element_type=jnp.float32
    )


def contracted_columns(left, right):
    return lax.dot_general(
        left, right, (((1,), (1,)), ((), ())), preferred_element_type=jnp.float32
    )


def per_device(
    frames, dilated_weight, dilated_bias, head_matrix, narrations, narration_counts, narration_spans
):
    present_tap = frames[0]
    length = present_tap.shape[0]
    narr_local = narrations.shape[0]
    preceding_tap = moved(present_tap, SHIFT_N)
    following_tap = moved(present_tap, -SHIFT_N)
    middle_frames = jnp.dot(present_tap, dilated_weight[1], preferred_element_type=jnp.float32)
    hidden_state = (
        middle_frames
        + jnp.dot(preceding_tap, dilated_weight[0], preferred_element_type=jnp.float32)
        + jnp.dot(following_tap, dilated_weight[2], preferred_element_type=jnp.float32)
        + dilated_bias
    )
    layer_out = (present_tap.astype(jnp.float32) + jnp.maximum(hidden_state, 0.0)).astype(
        jnp.bfloat16
    )
    embedded = jnp.dot(layer_out, head_matrix, preferred_element_type=jnp.float32).astype(
        jnp.bfloat16
    )
    every_narr = lax.all_gather(narrations, "video", axis=0, tiled=True)
    scores = logit_scale * contracted_columns(embedded, every_narr)
    slots = jnp.arange(narr_local, dtype=jnp.int32)
    valid = (slots[None, :] < narration_counts[:, None]).reshape(-1)
    masked = jnp.where(valid[None, :], scores, -jnp.inf)
    highest = jnp.max(masked, axis=1, keepdims=True)
    log_total = highest + jnp.log(jnp.sum(jnp.exp(masked - highest), axis=1, keepdims=True))
    video_index = lax.axis_index("video")
    own_count = lax.dynamic_index_in_dim(narration_counts, video_index, 0, keepdims=False)
    spans = narration_spans[0]
    positions = lax.axis_index("tm") * length + jnp.arange(length, dtype=jnp.int32)
    member = (
        (positions[:, None] >= spans[None, :, 0])
        & (positions[:, None] < spans[None, :, 1])
        & (slots[None, :] < own_count)
    ).astype(jnp.float32)
    labeled = jnp.sum(member, axis=1)
    own_start = video_index * narr_local
    own_scores = lax.dynamic_slice_in_dim(scores, own_start, narr_local, 1)
    local_loss = jnp.sum(labeled * log_total[:, 0]) - jnp.sum(member * own_scores)
    span_lengths = jnp.where(slots < own_count, spans[:, 1] - spans[:, 0], 0).astype(jnp.float32)
    label_total = lax.psum(jnp.sum(span_lengths), "video")
    factor = length * lax.axis_size("tm") * lax.axis_size("video") / label_total
    probs = jnp.exp(masked - log_total) * labeled[:, None]
    own_grad = lax.dynamic_slice_in_dim(probs, own_start, narr_local, 1) - member
    score_grad = lax.dynamic_update_slice_in_dim(probs, own_grad, own_start, 1)
    score_grad = (score_grad * factor).astype(jnp.bfloat16)
    embed_grad = (
        logit_scale * jnp.dot(score_grad, every_narr, preferred_element_type=jnp.float32)
    ).astype(jnp.bfloat16)
    head_resident = contracted_rows(layer_out, embed_grad)
    output_gradient = contracted_columns(embed_grad, head_matrix).astype(jnp.bfloat16)
    preactivation_gradient = jnp.where(
        hidden_state > 0.0, output_gradient.astype(jnp.float32), 0.0
    ).astype(jnp.bfloat16)
    received_following = moved_back(preactivation_gradient, -SHIFT_N)
    received_preceding = moved_back(preactivation_gradient, SHIFT_N)
    bias_local = jnp.sum(preactivation_gradient.astype(jnp.float32), axis=0)
    dilated_resident = jnp.stack(
        [
            contracted_rows(preceding_tap, preactivation_gradient),
            contracted_rows(present_tap, preactivation_gradient),
            contracted_rows(following_tap, preactivation_gradient),
        ]
    )
    input_gradient = (
        output_gradient.astype(jnp.float32)
        + contracted_columns(preactivation_gradient, dilated_weight[1])
        + contracted_columns(received_following, dilated_weight[0])
        + contracted_columns(received_preceding, dilated_weight[2])
    )
    loss_total, bias_overall = lax.psum((local_loss, bias_local), ("tm", "video"))
    dilated_complete, head_complete = lax.psum((dilated_resident, head_resident), "video")
    dilated_fraction, head_fraction = (
        lax.psum_scatter(dilated_complete, "tm", scatter_dimension=1, tiled=True),
        lax.psum_scatter(head_complete[None], "tm", scatter_dimension=1, tiled=True),
    )
    loss = loss_total / label_total
    return (
        loss,
        dilated_fraction,
        head_fraction[0],
        bias_overall,
        input_gradient.astype(jnp.bfloat16)[None],
    )


MESH = pl.DeviceIdType.MESH
F32, BF16 = jnp.float32, jnp.bfloat16


def section_kernel(
    n, videos, parts,
    counts_hbm, frames_hbm, weight_hbm, bias_hbm, head_hbm, narr_hbm, spans_hbm,
    dil_ref, head_out_ref, input_ref, bias_out_ref, loss_ref,
    counts_ref, frames_ref, weight_ref, bias_ref, head_ref, narr_ref, spans_ref, load_sem, turned, layer_out, embed_grad,
    earlier, later, narr_all, spans_all, hidden, out_grad, pre, pre_next, pre_prev,
    small_send, small_recv, edge_send, edge_recv, gather_send, gather_recv,
    small_ssem, small_rsem, *buffers,
):
    loads = [
        pltpu.make_async_copy(source, target, load_sem.at[k])
        for k, (source, target) in enumerate(
            (
                (frames_hbm, frames_ref), (weight_hbm, weight_ref), (bias_hbm, bias_ref), (spans_hbm, spans_ref),
                (counts_hbm, counts_ref), (head_hbm, head_ref), (narr_hbm, narr_ref),
            )
        )
    ]
    for copy in loads:
        copy.start()
    tm, vid = lax.axis_index("tm"), lax.axis_index("video")
    runs = n // 2
    core, row = lax.rem(vid, 2), lax.div(vid, 2)
    side, deep = lax.rem(tm, 2), lax.div(tm, 2)
    across_core = {"tm": tm, "video": vid + 1 - 2 * core}
    across_row = {"tm": tm, "video": lax.rem(vid + 2, videos)}
    across_side = {"tm": tm + 1 - 2 * side, "video": vid}

    def at_run(step):
        return {"tm": lax.rem(tm + 2 * step, n), "video": vid}

    def at_video(step):
        return {"tm": tm, "video": lax.rem(vid + step, videos)}

    barrier = pltpu.get_barrier_semaphore()
    peers = [across_side] + [at_run(s) for s in range(1, runs)] + [at_video(s) for s in range(1, videos)]
    for peer in peers:
        pl.semaphore_signal(barrier, inc=1, device_id=peer, device_id_type=MESH)
    pl.semaphore_wait(barrier, len(peers))

    def remote(src, dst, ssem, rsem, peer):
        return pltpu.make_async_remote_copy(
            src_ref=src, dst_ref=dst, send_sem=ssem, recv_sem=rsem, device_id=peer, device_id_type=MESH
        )

    has_prev, has_next = tm >= SHIFT_N, tm < n - SHIFT_N
    up = {"tm": lax.rem(tm + SHIFT_N, n), "video": vid}
    down = {"tm": lax.rem(tm + n - SHIFT_N, n), "video": vid}
    length = frames_hbm.shape[1]
    half = length // 2
    blocks = [pl.ds(0, half), pl.ds(half, half)]
    frames_up = [remote(frames_hbm.at[0, b], earlier.at[b], edge_send.at[k], edge_recv.at[k], up) for k, b in enumerate(blocks)]
    frames_down = [remote(frames_hbm.at[0, b], later.at[b], edge_send.at[2 + k], edge_recv.at[2 + k], down) for k, b in enumerate(blocks)]
    pre_up = [remote(pre.at[b], pre_prev.at[b], edge_send.at[4 + k], edge_recv.at[4 + k], up) for k, b in enumerate(blocks)]
    pre_down = [remote(pre.at[b], pre_next.at[b], edge_send.at[6 + k], edge_recv.at[6 + k], down) for k, b in enumerate(blocks)]
    for k in range(2):
        pl.when(has_next)(frames_up[k].start)
        pl.when(has_prev)(frames_down[k].start)
    gathers = []
    for step in range(1, videos):
        gathers.append(remote(spans_hbm, spans_all.at[step - 1], gather_send.at[0, step - 1], gather_recv.at[0, step - 1], at_video(step)))
        gathers.append(remote(narr_hbm, narr_all.at[step - 1], gather_send.at[1, step - 1], gather_recv.at[1, step - 1], at_video(step)))
    for copy in gathers:
        copy.start()

    def no_prev():
        earlier[...] = jnp.zeros_like(earlier)
        pre_prev[...] = jnp.zeros_like(pre_prev)

    def no_next():
        later[...] = jnp.zeros_like(later)
        pre_next[...] = jnp.zeros_like(pre_next)

    pl.when(jnp.logical_not(has_prev))(no_prev)
    pl.when(jnp.logical_not(has_next))(no_next)

    for copy in loads:
        copy.wait()
    present = frames_ref[0]
    turned[...] = present.T
    slots_count = narr_ref.shape[0]
    hidden[...] = jnp.dot(present, weight_ref[1], preferred_element_type=F32) + bias_ref[...]
    slots = lax.broadcasted_iota(jnp.int32, (1, slots_count), 1)
    starts, ends = spans_ref[0:1, :], spans_ref[1:2, :]
    own_live = slots < counts_ref[vid]
    lives = [own_live] + [slots < counts_ref[lax.rem(vid + videos - step, videos)] for step in range(1, videos)]
    local_loss = None
    for k, block in enumerate(blocks):
        positions = tm * length + k * half + lax.broadcasted_iota(jnp.int32, (half, 1), 0)
        member = ((positions >= starts) & (positions < ends) & own_live).astype(F32)
        labeled = jnp.sum(member, axis=1, keepdims=True)
        pl.when(has_prev)(frames_up[k].wait_recv)
        pl.when(has_next)(frames_down[k].wait_recv)
        state = (
            hidden[block]
            + jnp.dot(earlier[block], weight_ref[0], preferred_element_type=F32)
            + jnp.dot(later[block], weight_ref[2], preferred_element_type=F32)
        )
        layer = (frames_ref[0, block].astype(F32) + jnp.maximum(state, 0.0)).astype(BF16)
        layer_out[block] = layer
        embedded = jnp.dot(layer, head_ref[...], preferred_element_type=F32).astype(BF16)
        if k == 0:
            span_sum = jnp.where(own_live, (ends - starts).astype(F32), 0.0)
            for step in range(1, videos):
                gathers[2 * (step - 1)].wait_recv()
                gathers[2 * (step - 1) + 1].wait_recv()
                lengths = (spans_all[step - 1, 1:2, :] - spans_all[step - 1, 0:1, :]).astype(F32)
                span_sum = span_sum + jnp.where(lives[step], lengths, 0.0)
            label_total = jnp.sum(span_sum, axis=1, keepdims=True)
            factor = (length * n * videos) / label_total
        masked = []
        for step in range(videos):
            table = narr_all[step - 1] if step else narr_ref[...]
            scores = logit_scale * contracted_columns(embedded, table)
            if step == 0:
                own_scores = scores
            masked.append(jnp.where(lives[step], scores, -jnp.inf))
        highest = functools.reduce(jnp.maximum, [jnp.max(m, axis=1, keepdims=True) for m in masked])
        powers = [jnp.exp(m - highest) for m in masked]
        total = functools.reduce(jnp.add, [jnp.sum(e, axis=1, keepdims=True) for e in powers])
        log_total = highest + jnp.log(total)
        part_loss = jnp.sum(labeled * log_total, axis=0, keepdims=True) - jnp.sum(
            jnp.sum(member * own_scores, axis=1, keepdims=True), axis=0, keepdims=True
        )
        local_loss = part_loss if local_loss is None else local_loss + part_loss
        share = labeled / total
        embed_sum = None
        for step in range(videos):
            probs = powers[step] * share
            if step == 0:
                probs = probs - member
            table = narr_all[step - 1] if step else narr_ref[...]
            term = jnp.dot((probs * factor).astype(BF16), table, preferred_element_type=F32)
            embed_sum = term if embed_sum is None else embed_sum + term
        embed = (logit_scale * embed_sum).astype(BF16)
        embed_grad[block] = embed
        gradient = contracted_columns(embed, head_ref[...]).astype(BF16)
        out_grad[block] = gradient
        pre[block] = jnp.where(state > 0.0, gradient.astype(F32), 0.0).astype(BF16)
        pl.when(has_next)(pre_up[k].start)
        pl.when(has_prev)(pre_down[k].start)

    taps = (earlier, frames_ref.at[0], later)
    slabs = [buffers[13 * p:13 * (p + 1)] for p in range(len(parts))]
    band = slabs[0][0].shape[-2]

    def scatter(values, slab, first):
        accum, sent0 = slab[0], slab[1]
        width = values.shape[1]
        for z in range(runs):
            for x in range(2):
                for y in range(2):
                    for c in range(2):
                        at = (((z * 2 + x) * 2 + y) * 2 + c) * band
                        accum[c, y, x, z, :, first:first + width] = values[at:at + band]

    def send_first(slab):
        accum, sent0, recv0 = slab[0], slab[1], slab[2]
        sent0[...] = accum[1 - core].astype(BF16)
        copy = remote(sent0, recv0, slab[9].at[0], slab[10].at[0], across_core)
        copy.start()
        return copy

    first_copies = []
    for (pieces, order), slab in zip(parts, slabs):
        first = 0
        for tap, low, high in pieces:
            if tap == 3:
                values = contracted_rows(layer_out[...], embed_grad[:, low:high])
            elif tap == 1:
                values = jnp.dot(turned[...], pre[:, low:high], preferred_element_type=F32)
            else:
                values = contracted_rows(taps[tap][...], pre[:, low:high])
            scatter(values, slab, first)
            first += high - low
        first_copies.append(send_first(slab))

    bias_local = jnp.sum(pre[...].astype(F32), axis=0, keepdims=True)
    rows = lax.broadcasted_iota(jnp.int32, small_send.shape[1:], 0)
    small = jnp.where(rows == 0, bias_local, jnp.where(rows == 1, local_loss, 0.0))
    small_copies = []

    def small_start(index, peers_of):
        started = []
        for k, peer in enumerate(peers_of):
            copy = remote(small_send.at[index], small_recv.at[index + k], small_ssem.at[index + k], small_rsem.at[index + k], peer)
            copy.start()
            started.append(copy)
        small_copies.extend(started)
        return started

    small_send[0] = small
    small_now = small_start(0, [across_core])

    second_copies = []
    for (pieces, order), slab, copy in zip(parts, slabs, first_copies):
        accum, recv0, sent1, recv1 = slab[0], slab[2], slab[3], slab[4]
        copy.wait_recv()
        if order == "rows":
            for x in range(2):
                sent1[x] = (accum[core, 1 - row, x] + recv0[1 - row, x].astype(F32)).astype(BF16)
            peer = across_row
        else:
            for y in range(2):
                sent1[y] = (accum[core, y, 1 - side] + recv0[y, 1 - side].astype(F32)).astype(BF16)
            peer = across_side
        copy = remote(sent1, recv1, slab[9].at[1], slab[10].at[1], peer)
        copy.start()
        second_copies.append(copy)
    small_now[0].wait_recv()
    small = small + small_recv[0]
    small_send[1] = small
    small_now = small_start(1, [across_row])

    grad = out_grad[...].astype(F32) + contracted_columns(pre[...], weight_ref[1])
    for copy in pre_up:
        pl.when(has_prev)(copy.wait_recv)
    grad = grad + contracted_columns(pre_prev[...], weight_ref[2])
    for copy in pre_down:
        pl.when(has_next)(copy.wait_recv)
    grad = grad + contracted_columns(pre_next[...], weight_ref[0])
    input_ref[0] = grad.astype(BF16)

    third_copies = []
    for (pieces, order), slab, copy in zip(parts, slabs, second_copies):
        accum, recv0, recv1, sent2, recv2 = slab[0], slab[2], slab[4], slab[5], slab[6]
        copy.wait_recv()
        if order == "rows":
            sent2[...] = (accum[core, row, 1 - side] + recv0[row, 1 - side].astype(F32) + recv1[1 - side].astype(F32)).astype(BF16)
            peer = across_side
        else:
            sent2[...] = (accum[core, 1 - row, side] + recv0[1 - row, side].astype(F32) + recv1[1 - row].astype(F32)).astype(BF16)
            peer = across_row
        copy = remote(sent2, recv2, slab[9].at[2], slab[10].at[2], peer)
        copy.start()
        third_copies.append(copy)
    small_now[0].wait_recv()
    small = small + small_recv[1]
    small_send[2] = small
    small_now = small_start(2, [across_side])

    run_copies = []
    for (pieces, order), slab, copy in zip(parts, slabs, third_copies):
        accum, recv0, recv1, recv2, sent3, recv3 = slab[0], slab[2], slab[4], slab[6], slab[7], slab[8]
        copy.wait_recv()
        kept = recv1.at[side] if order == "rows" else recv1.at[row]
        started = []
        for step in range(1, runs):
            z = lax.rem(deep + step, runs)
            sent3[step] = (
                accum[core, row, side, z] + recv0[row, side, z].astype(F32) + kept[z].astype(F32) + recv2[z].astype(F32)
            ).astype(BF16)
            copy = remote(sent3.at[step], recv3.at[step], slab[9].at[2 + step], slab[10].at[2 + step], at_run(step))
            copy.start()
            started.append(copy)
        run_copies.append(started)
    small_now[0].wait_recv()
    small = small + small_recv[2]
    small_send[3] = small
    small_now = small_start(3, [at_run(s) for s in range(1, runs)])

    final_copies = []
    for (pieces, order), slab, started in zip(parts, slabs, run_copies):
        accum, recv0, recv1, recv2, recv3 = slab[0], slab[2], slab[4], slab[6], slab[8]
        final, fsend, frecv = slab[11], slab[9], slab[10]
        final_in = slab[12]
        kept = recv1.at[side] if order == "rows" else recv1.at[row]
        value = accum[core, row, side, deep] + recv0[row, side, deep].astype(F32) + kept[deep].astype(F32) + recv2[deep].astype(F32)
        for step in range(1, runs):
            started[step - 1].wait_recv()
            value = value + recv3[step].astype(F32)
        final[...] = value.astype(BF16)
        copies = []
        for step in range(1, videos):
            index = 1 + runs + step
            copy = remote(final, final_in.at[step - 1], fsend.at[index], frecv.at[index], at_video(step))
            copy.start()
            copies.append(copy)
        final_copies.append(copies)

    for copy in small_now:
        copy.wait_recv()
    total_small = None
    for z in range(runs):
        step = lax.rem(deep - z + runs, runs)
        term = small
        for s in range(1, runs):
            term = jnp.where(step == s, small_recv[2 + s], term)
        total_small = term if total_small is None else total_small + term
    bias_out_ref[...] = total_small[0:1]
    loss_ref[...] = total_small[1:2, 0:1] / label_total

    for (pieces, order), slab, copies in zip(parts, slabs, final_copies):
        for step in range(videos):
            if step:
                copies[step - 1].wait_recv()
                value = slab[12][step - 1]
            else:
                value = slab[11][...]
            value = value.astype(F32)
            at = pl.ds(pl.multiple_of(lax.rem(vid + videos - step, videos) * band, band), band)
            first = 0
            for tap, low, high in pieces:
                piece = value[:, first:first + high - low]
                if tap == 3:
                    head_out_ref[at, low:high] = piece
                else:
                    dil_ref[tap, at, low:high] = piece
                first += high - low

    for copy in frames_up + pre_up:
        pl.when(has_next)(copy.wait_send)
    for copy in frames_down + pre_down:
        pl.when(has_prev)(copy.wait_send)
    for copy in gathers + first_copies + small_copies + second_copies + third_copies:
        copy.wait_send()
    for started in run_copies + final_copies:
        for copy in started:
            copy.wait_send()


def write_kernel(*refs):
    sems = refs[10]
    copies = [pltpu.make_async_copy(refs[k], refs[5 + k], sems.at[k]) for k in range(5)]
    for copy in copies:
        copy.start()
    for copy in copies:
        copy.wait()


def section(n, videos, frames, dilated_weight, dilated_bias, head_matrix, narrations, narration_counts, narration_spans):
    length, channels = frames.shape[1:]
    width, slots = head_matrix.shape[1], narrations.shape[0]
    rows, runs = channels // n, n // 2
    band = rows // videos
    half, head_half = channels // 2, width // 2
    parts = (
        (((1, 0, channels),), "rows"),
        (((0, 0, channels),), "sides"),
        (((2, 0, half), (3, 0, head_half)), "rows"),
        (((2, half, channels), (3, head_half, width)), "sides"),
    )
    scratch = [
        pltpu.SMEM((videos,), jnp.int32),
        pltpu.VMEM((1, length, channels), BF16),
        pltpu.VMEM((3, channels, channels), BF16),
        pltpu.VMEM((1, channels), F32),
        pltpu.VMEM((channels, width), BF16),
        pltpu.VMEM((slots, width), BF16),
        pltpu.VMEM((2, slots), jnp.int32),
        pltpu.SemaphoreType.DMA((7,)),
        pltpu.VMEM((channels, length), BF16),
        pltpu.VMEM((length, channels), BF16),
        pltpu.VMEM((length, width), BF16),
        pltpu.VMEM((length, channels), BF16),
        pltpu.VMEM((length, channels), BF16),
        pltpu.VMEM((videos - 1, slots, width), BF16),
        pltpu.VMEM((videos - 1, 2, slots), jnp.int32),
        pltpu.VMEM((length, channels), F32),
        pltpu.VMEM((length, channels), BF16),
        pltpu.VMEM((length, channels), BF16),
        pltpu.VMEM((length, channels), BF16),
        pltpu.VMEM((length, channels), BF16),
        pltpu.VMEM((4, 8, channels), F32),
        pltpu.VMEM((2 + runs, 8, channels), F32),
        pltpu.SemaphoreType.DMA((8,)),
        pltpu.SemaphoreType.DMA((8,)),
        pltpu.SemaphoreType.DMA((2, videos - 1)),
        pltpu.SemaphoreType.DMA((2, videos - 1)),
        pltpu.SemaphoreType.DMA((2 + runs,)),
        pltpu.SemaphoreType.DMA((2 + runs,)),
    ]
    for pieces, order in parts:
        columns = sum(high - low for _, low, high in pieces)
        scratch += [
            pltpu.VMEM((2, 2, 2, runs, band, columns), F32),
            pltpu.VMEM((2, 2, runs, band, columns), BF16),
            pltpu.VMEM((2, 2, runs, band, columns), BF16),
            pltpu.VMEM((2, runs, band, columns), BF16),
            pltpu.VMEM((2, runs, band, columns), BF16),
            pltpu.VMEM((runs, band, columns), BF16),
            pltpu.VMEM((runs, band, columns), BF16),
            pltpu.VMEM((runs, band, columns), BF16),
            pltpu.VMEM((runs, band, columns), BF16),
            pltpu.SemaphoreType.DMA((1 + runs + videos,)),
            pltpu.SemaphoreType.DMA((1 + runs + videos,)),
            pltpu.VMEM((band, columns), BF16),
            pltpu.VMEM((videos - 1, band, columns), BF16),
        ]
    vmem, hbm = pl.BlockSpec(memory_space=pltpu.VMEM), pl.BlockSpec(memory_space=pltpu.HBM)
    shapes = (
        jax.ShapeDtypeStruct((3, rows, channels), F32),
        jax.ShapeDtypeStruct((rows, width), F32),
        jax.ShapeDtypeStruct((1, length, channels), BF16),
        jax.ShapeDtypeStruct((1, channels), F32),
        jax.ShapeDtypeStruct((1, 1), F32),
    )
    results = pl.pallas_call(
        functools.partial(section_kernel, n, videos, parts),
        out_shape=shapes,
        in_specs=[hbm] * 7,
        out_specs=(vmem,) * 5,
        scratch_shapes=scratch,
        compiler_params=pltpu.CompilerParams(
            collective_id=0, has_side_effects=True, vmem_limit_bytes=48 * 1024 * 1024
        ),
    )(
        *(
            pltpu.with_memory_space_constraint(array, pltpu.HBM)
            for array in (
                narration_counts, frames, dilated_weight, dilated_bias[None], head_matrix, narrations,
                narration_spans[0].T,
            )
        )
    )
    dil, head, inputs, bias, loss = pl.pallas_call(
        write_kernel,
        out_shape=shapes,
        in_specs=[vmem] * 5,
        out_specs=(hbm,) * 5,
        scratch_shapes=[pltpu.SemaphoreType.DMA((5,))],
        compiler_params=pltpu.CompilerParams(vmem_limit_bytes=1024 * 1024),
    )(*results)
    return loss[0, 0], dil, head, bias[0], inputs


def solution(mesh):
    n, videos = mesh.shape["tm"], mesh.shape["video"]

    def body(*arrays):
        frames, weight = arrays[0], arrays[1]
        if videos == 4 and n % 4 == 0 and weight.shape[1] % (16 * n * videos) == 0:
            return section(n, videos, *arrays)
        return per_device(*arrays)

    return jax.shard_map(
        body,
        mesh=mesh,
        in_specs=(
            P("video", "tm", None),
            P(),
            P(),
            P(),
            P("video", None),
            P(),
            P("video", None, None),
        ),
        out_specs=(P(), P(None, "tm", None), P("tm", None), P(), P("video", "tm", None)),
        check_vma=False,
    )
```
